32 devices in a mesh: dp: 16 (over z, y, x), rep: 2 (over core).
Axes of the slice: x: 2, y: 2, z: 4, core: 2. Of those that a mesh axis runs over, the one named last changes fastest.
Arguments:
- queries: bfloat16 [24576, 256], P(('dp', 'rep')), may hold values from -100 to 100
- candidates: bfloat16 [24576, 256], P(('dp', 'rep')), may hold values from -6 to 6
- bucket: int32 [24576, 1], P(('dp', 'rep')), may hold values from 0 to 15, as said below
Outputs:
- query_loss: float32 [24576], P(('dp', 'rep'))
- bucket_loss: float32 [16], P('dp')
The draws below stay inside these ranges and needn't reach their ends.
Inputs may be any that keep to these rules, and one draw needn't show every extreme that they name: The 768 rows of one device name any bucket at most 96 times; on some device some bucket is named exactly 96 times; a bucket may be named by no row at all.
All inputs are finite; a program needn't handle non-finite values.
Results may differ from the reference program's by a relative error of at most 0.0003.
Values may be sent and summed in bfloat16 or wider, within the bound.
A program may use at most 64 MiB of HBM per device.

```python
import jax
import jax.numpy as jnp
from jax import lax

E = 256
TOK_DEV = 768
CAP = 96
TOKENS = 24576
N_DP = 16
N_REP = 2


def shared_candidates(key):
    rows = jax.random.normal(jax.random.fold_in(key, 101), (TOKENS, E), jnp.float32)
    return jnp.clip(rows, -6.0, 6.0)


def draw_candidates(key, part):
    return shared_candidates(key).astype(jnp.bfloat16)


def draw_queries(key, part):
    base = jnp.clip(jax.random.normal(jax.random.fold_in(key, 202), (TOKENS, E), jnp.float32), -6.0, 6.0)
    return base.astype(jnp.bfloat16)


def draw_bucket(key, part):
    devices = TOKENS // TOK_DEV
    hot_count = max(1, N_DP // 32)
    order = jax.random.permutation(jax.random.fold_in(key, 11), N_DP).astype(jnp.int32)
    hot_rows = jnp.repeat(order[2:2 + hot_count], CAP)
    pool = jnp.repeat(order[2 + hot_count:], CAP)
    extra = TOK_DEV - hot_count * CAP

    def one_device(index):
        device_key = jax.random.fold_in(jax.random.fold_in(key, 23), index)
        picked = jax.random.permutation(device_key, pool)[:extra]
        rows = jnp.concatenate([hot_rows, picked], axis=0)
        return jax.random.permutation(jax.random.fold_in(device_key, 5), rows)
    blocks = jax.vmap(one_device)(jnp.arange(devices, dtype=jnp.int32))
    return blocks.reshape(TOKENS, 1).astype(jnp.int32)


def setup_inputs(seed: int = 0) -> dict:
    key_of = jax.random.split(jax.random.key(seed), 4)
    return {
        "queries": draw_queries(jax.random.fold_in(key_of[3], 71), 0),
        "candidates": draw_candidates(jax.random.fold_in(key_of[3], 71), 0),
        "bucket": draw_bucket(jax.random.fold_in(key_of[3], 71), 0),
    }


score_scale = 0.0625
neg_large = -1.0e30


def reference(queries, candidates, bucket):
    ids = bucket[:, 0].astype(jnp.int32)
    order = jnp.argsort(ids, stable=True).astype(jnp.int32)
    span = N_REP * N_DP * CAP
    sorted_q = jnp.concatenate([queries[order].astype(jnp.float32), jnp.zeros((span, E), jnp.float32)], axis=0)
    sorted_c = jnp.concatenate([candidates[order].astype(jnp.float32), jnp.zeros((span, E), jnp.float32)], axis=0)
    order_pad = jnp.concatenate([order, jnp.full((span,), TOKENS, jnp.int32)], axis=0)
    counts = jnp.zeros((N_DP,), jnp.int32).at[ids].add(jnp.ones((TOKENS,), jnp.int32)).astype(jnp.int32)
    starts = (jnp.cumsum(counts) - counts).astype(jnp.int32)

    def one_bucket(item):
        start, count = item
        qrows = lax.dynamic_slice_in_dim(sorted_q, start, span, 0)
        crows = lax.dynamic_slice_in_dim(sorted_c, start, span, 0)
        where_idx = lax.dynamic_slice_in_dim(order_pad, start, span, 0)
        valid = jnp.arange(span, dtype=jnp.int32) < count
        scores = jnp.dot(qrows, crows.T, precision=lax.Precision.HIGHEST) * score_scale
        scores = jnp.where(valid[None, :], scores, neg_large)
        top = jnp.max(scores, axis=1)
        lse = top + jnp.log(jnp.sum(jnp.exp(scores - top[:, None]), axis=1))
        pos = jnp.sum(qrows * crows, axis=1) * score_scale
        count_safe = jnp.maximum(count.astype(jnp.float32), 1.0)
        loss = jnp.where(valid, lse - jnp.log(count_safe) - pos, 0.0)
        idx = jnp.where(valid, where_idx, TOKENS).astype(jnp.int32)
        return loss, idx, jnp.sum(loss) / count_safe

    losses, indices, bucket_loss = lax.map(one_bucket, (starts, counts))
    query_loss = jnp.zeros((TOKENS,), jnp.float32).at[indices.reshape(-1)].set(losses.reshape(-1), mode="drop")
    return query_loss, bucket_loss
```

```python
import functools
import math

import jax
import jax.numpy as jnp
from jax import lax
from jax.experimental import pallas as pl
from jax.experimental.pallas import tpu as pltpu
from jax.sharding import PartitionSpec as P

MESH = pl.DeviceIdType.MESH
score_scale = 0.0625
neg_large = -1e30
log2e = math.log2(math.e)


def xor(a, b, n):
    out, bit = 0, 1
    while bit < n:
        out = out + bit * ((a // bit + b // bit) % 2)
        bit *= 2
    return out


def kernel(
    n, cap, b_ref, q_ref, c_ref, ql_ref, bl_ref,
    slot_buf, hot_buf, rank_buf, bias_buf, s_buf,
    qs, cs, qr, cr, co, vs, vr, vo, ls, lr, xs, xr,
    c_ss, c_rs, q_ss, q_rs, v_ss, v_rs, l_ss, l_rs, f_ss, f_rs, x_ss, x_rs,
):
    me = lax.axis_index("dp")
    rep = lax.axis_index("rep")
    partner = (me, 1 - rep)
    rows, width = q_ref.shape
    slots = n * cap

    barrier = pltpu.get_barrier_semaphore()

    def greet(k, carry):
        pl.semaphore_signal(
            barrier, inc=1, device_id=(xor(me, k, n), rep), device_id_type=MESH
        )
        return carry

    lax.fori_loop(1, n, greet, 0)
    pl.semaphore_signal(barrier, inc=1, device_id=partner, device_id_type=MESH)

    hot = (b_ref[...] == lax.broadcasted_iota(jnp.int32, (rows, n), 1)).astype(jnp.bfloat16)
    first = lax.broadcasted_iota(jnp.int32, (rows, rows), 0)
    second = lax.broadcasted_iota(jnp.int32, (rows, rows), 1)
    before = (first < second).astype(jnp.bfloat16)
    same = (first == second).astype(jnp.bfloat16)
    dims = (((0,), (0,)), ((), ()))
    ahead = lax.dot_general(hot, before, dims, preferred_element_type=jnp.float32)
    hot_t = lax.dot_general(hot, same, dims, preferred_element_type=jnp.float32)
    owner_col = lax.broadcasted_iota(jnp.int32, (n, rows), 0).astype(jnp.float32)
    rank = jnp.sum(hot_t * ahead, axis=0, keepdims=True)
    base = jnp.sum(hot_t * owner_col, axis=0, keepdims=True) * cap
    hot_buf[...] = hot_t
    rank_buf[...] = rank.astype(jnp.int32)
    slot_buf[...] = (base + rank).astype(jnp.int32)
    counts = jnp.sum(hot_t, axis=1, keepdims=True)
    vs[:, 0, :] = jnp.broadcast_to(counts, (n, 128))

    pl.semaphore_wait(barrier, n)

    def remote(src, dst, ss, rs, device):
        return pltpu.make_async_remote_copy(
            src_ref=src, dst_ref=dst, send_sem=ss, recv_sem=rs,
            device_id=device, device_id_type=MESH,
        )

    def v_copy(o):
        return remote(vs.at[o], vr.at[me], v_ss.at[o], v_rs.at[me], (o, rep))

    def c_copy(o):
        return remote(cs.at[o], cr.at[me], c_ss.at[o], c_rs.at[me], (o, rep))

    def q_copy(o):
        return remote(qs.at[o], qr.at[me], q_ss.at[o], q_rs.at[me], (o, rep))

    def l_copy(o):
        return remote(ls.at[o], lr.at[me], l_ss.at[o], l_rs.at[me], (o, rep))

    def f_copy(o):
        return remote(cr.at[o], co.at[o], f_ss.at[o], f_rs.at[o], partner)

    def v_from(o):
        return remote(vs.at[me], vr.at[o], v_ss.at[o], v_rs.at[o], (o, rep))

    def c_from(o):
        return remote(cs.at[me], cr.at[o], c_ss.at[o], c_rs.at[o], (o, rep))

    def q_from(o):
        return remote(qs.at[me], qr.at[o], q_ss.at[o], q_rs.at[o], (o, rep))

    def l_from(o):
        return remote(ls.at[me], lr.at[o], l_ss.at[o], l_rs.at[o], (o, rep))

    within = lax.broadcasted_iota(jnp.int32, (cap, rows), 0)

    def pick(o, x_ref):
        chosen = (slot_buf[...] == within + o * cap).astype(jnp.bfloat16)
        return jnp.dot(chosen, x_ref[...], preferred_element_type=jnp.float32).astype(
            jnp.bfloat16
        )

    cs[xor(me, n - 1, n)] = pick(xor(me, n - 1, n), c_ref)

    def pack_c(t, carry):
        k = n - 1 - t
        nxt = xor(me, k - 1, n)
        cs[nxt] = pick(nxt, c_ref)
        o = xor(me, k, n)
        c_copy(o).start()
        v_copy(o).start()
        return carry

    lax.fori_loop(0, n - 1, pack_c, 0)
    cr[me] = cs[me]
    vr[me] = vs[me]

    qs[xor(me, n - 1, n)] = pick(xor(me, n - 1, n), q_ref)

    def pack_q(t, carry):
        k = n - 1 - t
        nxt = xor(me, k - 1, n)
        qs[nxt] = pick(nxt, q_ref)
        q_copy(xor(me, k, n)).start()
        return carry

    lax.fori_loop(0, n - 1, pack_q, 0)
    qr[me] = qs[me]
    f_copy(me).start()

    def forward(t, carry):
        o = xor(me, n - 1 - t, n)
        c_from(o).wait_recv()
        f_copy(o).start()
        v_from(o).wait_recv()
        return carry

    lax.fori_loop(0, n - 1, forward, 0)
    v_forward = remote(vr, vo, x_ss.at[0], x_rs.at[0], partner)
    v_forward.start()
    v_forward.wait_recv()

    spread = (
        lax.broadcasted_iota(jnp.int32, (n, slots), 0)
        == lax.broadcasted_iota(jnp.int32, (n, slots), 1) // cap
    ).astype(jnp.bfloat16)
    place = lax.broadcasted_iota(jnp.int32, (1, slots), 1) % cap
    mine, other = vr[:, 0, :], vo[:, 0, :]
    for half, held in enumerate((mine, other)):
        number = lax.dot_general(
            held.astype(jnp.bfloat16), spread, dims, preferred_element_type=jnp.float32
        )[0:1]
        bias_buf[:, half * slots : (half + 1) * slots] = jnp.where(
            place.astype(jnp.float32) < number, 0.0, neg_large
        )
    count = jnp.sum(mine, axis=0, keepdims=True) + jnp.sum(other, axis=0, keepdims=True)
    count_safe = jnp.maximum(count, 1.0)
    log_count = jnp.log(count_safe)

    def landed(t, carry):
        f_copy(xor(me, n - 1 - t, n)).wait_recv()
        return carry

    lax.fori_loop(0, n, landed, 0)

    chunk = math.gcd(slots, 256)
    row_at = lax.broadcasted_iota(jnp.int32, (cap, 128), 0)
    lane_at = lax.broadcasted_iota(jnp.int32, (cap, 128), 1)
    diagonal = row_at == lane_at
    row_number = row_at.astype(jnp.float32)

    def block_loss(j):
        block = qr[j]
        top = jnp.full((cap, 128), neg_large, jnp.float32)
        for half, held in enumerate((cr, co)):
            flat = held.reshape(slots, width)
            for start in range(0, slots, chunk):
                at = half * slots + start
                scores = lax.dot_general(
                    block, flat[start : start + chunk, :],
                    (((1,), (1,)), ((), ())), preferred_element_type=jnp.float32,
                ) + bias_buf[:, at : at + chunk]
                s_buf[:, at : at + chunk] = scores
                for lane in range(0, chunk, 128):
                    top = jnp.maximum(top, scores[:, lane : lane + 128])
        peak = jnp.max(top, axis=1, keepdims=True)
        wide = jnp.broadcast_to(peak, (cap, 128))
        total = jnp.zeros((cap, 128), jnp.float32)
        for at in range(0, 2 * slots, 128):
            total = total + jnp.exp2((s_buf[:, at : at + 128] - wide) * (score_scale * log2e))
        lse = peak * score_scale + jnp.log(jnp.sum(total, axis=1, keepdims=True))
        positive = score_scale * jnp.sum(
            block.astype(jnp.float32) * cr[j].astype(jnp.float32), axis=1, keepdims=True
        )
        loss = (lse - positive) - log_count
        keep = jnp.logical_and(diagonal, row_number < vr[j])
        return jnp.sum(jnp.where(keep, loss, 0.0), axis=0, keepdims=True)

    mine_row = block_loss(me)
    lr[me] = mine_row

    def step(t, total):
        j = xor(me, n - 1 - t, n)
        q_from(j).wait_recv()
        row = block_loss(j)
        ls[j] = row
        total = total + row
        xs[...] = total
        l_copy(j).start()
        return total

    total = lax.fori_loop(0, n - 1, step, mine_row)
    x_copy = remote(xs, xr, x_ss.at[1], x_rs.at[1], partner)
    x_copy.start()

    def close(t, carry):
        o = xor(me, n - 1 - t, n)
        c_copy(o).wait_send()
        q_copy(o).wait_send()
        v_copy(o).wait_send()
        l_copy(o).wait_send()
        f_copy(o).wait_send()
        l_from(o).wait_recv()
        return carry

    lax.fori_loop(0, n - 1, close, 0)
    f_copy(me).wait_send()
    v_forward.wait_send()

    spread_loss = lax.dot_general(
        lr[:, 0, :], hot_buf[...], dims,
        precision=lax.Precision.HIGHEST, preferred_element_type=jnp.float32,
    )
    here = lax.broadcasted_iota(jnp.int32, (128, rows), 0) == rank_buf[...]
    ql_ref[...] = jnp.sum(jnp.where(here, spread_loss, 0.0), axis=0, keepdims=True)
    x_copy.wait()
    summed = jnp.sum(total + xr[...], axis=1, keepdims=True)
    bl_ref[...] = summed / count_safe


def shards(queries, candidates, bucket):
    n = lax.axis_size("dp")
    rows, width = queries.shape
    cap = max(2, 2 * rows // n)
    cap = (cap + 15) // 16 * 16
    slots = n * cap
    bf16, f32 = jnp.bfloat16, jnp.float32
    vmem = pl.BlockSpec(memory_space=pltpu.VMEM)
    dma = pltpu.SemaphoreType.DMA
    query_loss, bucket_loss = pl.pallas_call(
        functools.partial(kernel, n, cap),
        out_shape=(
            jax.ShapeDtypeStruct((1, rows), f32),
            jax.ShapeDtypeStruct((1, 128), f32),
        ),
        in_specs=[vmem] * 3,
        out_specs=(vmem, vmem),
        scratch_shapes=[
            pltpu.VMEM((1, rows), jnp.int32),
            pltpu.VMEM((n, rows), f32),
            pltpu.VMEM((1, rows), jnp.int32),
            pltpu.VMEM((1, 2 * slots), f32),
            pltpu.VMEM((cap, 2 * slots), f32),
            pltpu.VMEM((n, cap, width), bf16),
            pltpu.VMEM((n, cap, width), bf16),
            pltpu.VMEM((n, cap, width), bf16),
            pltpu.VMEM((n, cap, width), bf16),
            pltpu.VMEM((n, cap, width), bf16),
            pltpu.VMEM((n, 1, 128), f32),
            pltpu.VMEM((n, 1, 128), f32),
            pltpu.VMEM((n, 1, 128), f32),
            pltpu.VMEM((n, 1, 128), f32),
            pltpu.VMEM((n, 1, 128), f32),
            pltpu.VMEM((1, 128), f32),
            pltpu.VMEM((1, 128), f32),
        ]
        + [dma((n,))] * 10
        + [dma((2,))] * 2,
        compiler_params=pltpu.CompilerParams(collective_id=0, has_side_effects=True),
        name="bucket_loss",
    )(bucket, queries, candidates)
    return query_loss.reshape(rows), bucket_loss[0, :1]


def solution(mesh):
    in_specs = (P(("dp", "rep"), None), P(("dp", "rep"), None), P(("dp", "rep"), None))
    out_specs = (P(("dp", "rep")), P("dp"))
    return jax.shard_map(shards, mesh=mesh, in_specs=in_specs, out_specs=out_specs, check_vma=False)
```

```python
import functools
import math

import jax
import jax.numpy as jnp
from jax import lax
from jax.experimental import pallas as pl
from jax.experimental.pallas import tpu as pltpu
from jax.sharding import PartitionSpec as P

MESH = pl.DeviceIdType.MESH
score_scale = 0.0625
neg_large = -1e30
log2e = math.log2(math.e)


def xor(a, b, n):
    out, bit = 0, 1
    while bit < n:
        out = out + bit * ((a // bit + b // bit) % 2)
        bit *= 2
    return out


def kernel(
    n, cap, group, b_ref, q_ref, c_ref, ql_ref, bl_ref,
    slot_buf, hot_buf, rank_buf, bias_buf, s_buf,
    qs, cs, qr, cr, co, vs, vr, vo, ls, lr, xs, xr,
    c_ss, c_rs, q_ss, q_rs, v_ss, v_rs, l_ss, l_rs, f_ss, f_rs, x_ss, x_rs,
):
    me = lax.axis_index("dp")
    rep = lax.axis_index("rep")
    partner = (me, 1 - rep)
    rows, width = q_ref.shape
    slots = n * cap
    lanes = group * cap
    groups = n // group
    quarter = n // 4
    zone = me // quarter
    middle = (zone * (3 - zone)) // 2

    barrier = pltpu.get_barrier_semaphore()

    def greet(k, carry):
        pl.semaphore_signal(
            barrier, inc=1, device_id=(xor(me, k, n), rep), device_id_type=MESH
        )
        return carry

    lax.fori_loop(1, n, greet, 0)
    pl.semaphore_signal(barrier, inc=1, device_id=partner, device_id_type=MESH)

    owner_col = lax.broadcasted_iota(jnp.int32, (n, rows), 0)
    chosen = owner_col == b_ref[...]
    hot = jnp.where(chosen, 1.0, 0.0)
    before = (
        lax.broadcasted_iota(jnp.int32, (rows, rows), 0)
        < lax.broadcasted_iota(jnp.int32, (rows, rows), 1)
    ).astype(jnp.bfloat16)
    dims = (((0,), (0,)), ((), ()))
    ahead = jnp.dot(hot.astype(jnp.bfloat16), before, preferred_element_type=jnp.float32)
    rank = jnp.sum(hot * ahead, axis=0, keepdims=True).astype(jnp.int32)
    hot_buf[...] = hot
    rank_buf[...] = rank
    slot_buf[...] = b_ref[...] * cap + rank
    vs[:, 0, :] = jnp.broadcast_to(jnp.sum(hot, axis=1, keepdims=True), (n, lanes))

    def remote(src, dst, ss, rs, device):
        return pltpu.make_async_remote_copy(
            src_ref=src, dst_ref=dst, send_sem=ss, recv_sem=rs,
            device_id=device, device_id_type=MESH,
        )

    def v_copy(o):
        return remote(vs.at[o], vr.at[me], v_ss.at[o], v_rs.at[me], (o, rep))

    def c_copy(o):
        return remote(cs.at[o], cr.at[me], c_ss.at[o], c_rs.at[me], (o, rep))

    def q_copy(o):
        return remote(qs.at[o], qr.at[me], q_ss.at[o], q_rs.at[me], (o, rep))

    def l_copy(o):
        return remote(ls.at[o // group], lr.at[me], l_ss.at[o], l_rs.at[me], (o, rep))

    def f_copy(o):
        return remote(cr.at[o], co.at[o], f_ss.at[o], f_rs.at[o], partner)

    def v_from(o):
        return remote(vs.at[me], vr.at[o], v_ss.at[o], v_rs.at[o], (o, rep))

    def c_from(o):
        return remote(cs.at[me], cr.at[o], c_ss.at[o], c_rs.at[o], (o, rep))

    def q_from(o):
        return remote(qs.at[me], qr.at[o], q_ss.at[o], q_rs.at[o], (o, rep))

    def l_from(o):
        return remote(ls.at[0], lr.at[o], l_ss.at[o], l_rs.at[o], (o, rep))

    within = lax.broadcasted_iota(jnp.int32, (cap, rows), 0)

    def pick(o, x_ref):
        taken = (slot_buf[...] == within + o * cap).astype(jnp.bfloat16)
        return jnp.dot(taken, x_ref[...], preferred_element_type=jnp.float32).astype(
            jnp.bfloat16
        )

    def peer(t):
        near = quarter + (t + middle * quarter) % (3 * quarter)
        inside = (t + 1) % quarter
        apart = t // (3 * quarter)
        return xor(me, near * (1 - apart) + inside * apart, n)

    def arrival(u, size):
        return size + (u + middle * 2 * size) % (3 * size)

    cs[peer(0)] = pick(peer(0), c_ref)
    pl.semaphore_wait(barrier, n)

    def pack_c(t, carry):
        nxt = peer(t + 1)
        cs[nxt] = pick(nxt, c_ref)
        o = peer(t)
        c_copy(o).start()
        v_copy(o).start()
        return carry

    lax.fori_loop(0, n - 1, pack_c, 0)
    cr[me] = cs[me]
    vr[me] = vs[me]

    qs[peer(0)] = pick(peer(0), q_ref)

    def pack_q(t, carry):
        nxt = peer(t + 1)
        qs[nxt] = pick(nxt, q_ref)
        q_copy(peer(t)).start()
        return carry

    lax.fori_loop(0, n - 1, pack_q, 0)
    qr[me] = qs[me]
    f_copy(me).start()

    row_at = lax.broadcasted_iota(jnp.int32, (cap, lanes), 0)
    lane_at = lax.broadcasted_iota(jnp.int32, (cap, lanes), 1)
    row_number = row_at.astype(jnp.float32)

    def fill_bias(number, at):
        bias_buf[pl.ds(pl.multiple_of(at, cap), cap), :] = jnp.where(
            row_number < number, 0.0, neg_large
        )

    def forward(o):
        c_from(o).wait_recv()
        f_copy(o).start()
        v_from(o).wait_recv()

    lax.fori_loop(1, quarter, lambda k, c: (forward(xor(me, k, n)), c)[1], 0)
    lax.fori_loop(
        0, 3 * quarter, lambda u, c: (forward(xor(me, arrival(u, quarter), n)), c)[1], 0
    )
    v_forward = remote(vr, vo, x_ss.at[0], x_rs.at[0], partner)
    v_forward.start()
    lax.fori_loop(0, n, lambda j, c: (fill_bias(vr[j], j * cap), c)[1], 0)
    v_forward.wait_recv()
    lax.fori_loop(0, n, lambda j, c: (fill_bias(vo[j], (n + j) * cap), c)[1], 0)
    count = jnp.sum(vr[:, 0, :], axis=0, keepdims=True) + jnp.sum(
        vo[:, 0, :], axis=0, keepdims=True
    )
    count_safe = jnp.maximum(count, 1.0)
    log_count = jnp.log(count_safe)
    lax.fori_loop(0, n, lambda j, c: (f_copy(j).wait_recv(), c)[1], 0)

    chunk = math.gcd(slots, 256)
    one_row = lax.broadcasted_iota(jnp.int32, (1, lanes), 1)

    def group_loss(p):
        block = qr[pl.ds(p * group, group)].reshape(lanes, width)
        top = jnp.full((8, lanes), neg_large, jnp.float32)
        for half, held in enumerate((cr, co)):
            flat = held.reshape(slots, width)
            for start in range(0, slots, chunk):
                at = half * slots + start
                scores = lax.dot_general(
                    flat[start : start + chunk, :], block,
                    (((1,), (1,)), ((), ())), preferred_element_type=jnp.float32,
                ) + bias_buf[at : at + chunk, :]
                s_buf[at : at + chunk, :] = scores
                top = jnp.maximum(top, jnp.max(scores.reshape(chunk // 8, 8, lanes), axis=0))
        peak = jnp.max(top, axis=0, keepdims=True)
        total = jnp.zeros((8, lanes), jnp.float32)
        for at in range(0, 2 * slots, chunk):
            powers = jnp.exp2((s_buf[at : at + chunk, :] - peak) * (score_scale * log2e))
            total = total + jnp.sum(powers.reshape(chunk // 8, 8, lanes), axis=0)
        lse = peak * score_scale + jnp.log(jnp.sum(total, axis=0, keepdims=True))
        positive = jnp.zeros((1, lanes), jnp.float32)
        keep = jnp.zeros((1, lanes), jnp.float32)
        for g in range(group):
            j = p * group + g
            own = s_buf[pl.ds(pl.multiple_of(j * cap, cap), cap), :]
            positive = positive + jnp.sum(
                jnp.where(row_at == lane_at - g * cap, own, 0.0), axis=0, keepdims=True
            )
            place = one_row - g * cap
            here = jnp.logical_and(place >= 0, place.astype(jnp.float32) < vr[j])
            here = jnp.logical_and(here, place < cap)
            keep = jnp.where(here, 1.0, keep)
        loss = (lse - positive * score_scale) - log_count
        return jnp.where(keep > 0.0, loss, 0.0)

    def step(m, total):
        p = xor(me // group, m, groups)
        for g in range(group):
            j = p * group + g

            @pl.when(j != me)
            def _():
                q_from(j).wait_recv()

        row = group_loss(p)
        ls[p] = row
        total = total + row
        xs[...] = total
        for g in range(group):
            j = p * group + g

            @pl.when(j != me)
            def _():
                l_copy(j).start()

        return total

    part = groups // 4
    total = lax.fori_loop(0, part, step, jnp.zeros((1, lanes), jnp.float32))
    total = lax.fori_loop(0, 3 * part, lambda u, c: step(arrival(u, part), c), total)
    lr[me] = ls[me // group]
    x_copy = remote(xs, xr, x_ss.at[1], x_rs.at[1], partner)
    x_copy.start()

    def close(t, carry):
        o = xor(me, n - 1 - t, n)
        c_copy(o).wait_send()
        q_copy(o).wait_send()
        v_copy(o).wait_send()
        l_copy(o).wait_send()
        f_copy(o).wait_send()
        l_from(o).wait_recv()
        return carry

    lax.fori_loop(0, n - 1, close, 0)
    f_copy(me).wait_send()
    v_forward.wait_send()

    spread_loss = lax.dot_general(
        lr[:, 0, :], hot_buf[...], dims,
        precision=lax.Precision.HIGHEST, preferred_element_type=jnp.float32,
    )
    mine = lax.broadcasted_iota(jnp.int32, (lanes, rows), 0) == rank_buf[...] + (me % group) * cap
    ql_ref[...] = jnp.sum(jnp.where(mine, spread_loss, 0.0), axis=0)
    x_copy.wait()
    summed = jnp.sum(total + xr[...], axis=1, keepdims=True)
    bl_ref[...] = (summed / count_safe)[:, :128]


def shards(queries, candidates, bucket):
    n = lax.axis_size("dp")
    rows, width = queries.shape
    cap = max(2, 2 * rows // n)
    cap = (cap + 15) // 16 * 16
    group = 1
    while 2 * group * cap <= 256 and n % (8 * group) == 0:
        group *= 2
    slots, lanes = n * cap, group * cap
    bf16, f32 = jnp.bfloat16, jnp.float32
    vmem = pl.BlockSpec(memory_space=pltpu.VMEM)
    dma = pltpu.SemaphoreType.DMA
    query_loss, bucket_loss = pl.pallas_call(
        functools.partial(kernel, n, cap, group),
        out_shape=(
            jax.ShapeDtypeStruct((rows,), f32),
            jax.ShapeDtypeStruct((1, 128), f32),
        ),
        in_specs=[vmem] * 3,
        out_specs=(vmem, vmem),
        scratch_shapes=[
            pltpu.VMEM((1, rows), jnp.int32),
            pltpu.VMEM((n, rows), f32),
            pltpu.VMEM((1, rows), jnp.int32),
            pltpu.VMEM((2 * slots, lanes), f32),
            pltpu.VMEM((2 * slots, lanes), f32),
        ]
        + [pltpu.VMEM((n, cap, width), bf16)] * 5
        + [pltpu.VMEM((n, 1, lanes), f32)] * 3
        + [pltpu.VMEM((n // group, 1, lanes), f32), pltpu.VMEM((n, 1, lanes), f32)]
        + [pltpu.VMEM((1, lanes), f32)] * 2
        + [dma((n,))] * 10
        + [dma((2,))] * 2,
        compiler_params=pltpu.CompilerParams(collective_id=0, has_side_effects=True),
        name="bucket_loss",
    )(bucket.reshape(1, rows), queries, candidates)
    return query_loss, bucket_loss[0, :1]


def solution(mesh):
    in_specs = (P(("dp", "rep"), None), P(("dp", "rep"), None), P(("dp", "rep"), None))
    out_specs = (P(("dp", "rep")), P("dp"))
    return jax.shard_map(shards, mesh=mesh, in_specs=in_specs, out_specs=out_specs, check_vma=False)
```

```python
import functools
import math

import jax
import jax.numpy as jnp
from jax import lax
from jax.experimental import pallas as pl
from jax.experimental.pallas import tpu as pltpu
from jax.sharding import PartitionSpec as P

MESH = pl.DeviceIdType.MESH
score_scale = 0.0625
neg_large = -1e30
log2e = math.log2(math.e)


def xor(a, b, n):
    out, bit = 0, 1
    while bit < n:
        out = out + bit * ((a // bit + b // bit) % 2)
        bit *= 2
    return out


def kernel(
    n, cap, group, b_hbm, q_hbm, c_hbm, ql_ref, bl_ref, b_ref, q_ref, c_ref,
    slot_buf, hot_buf, rank_buf, bias_buf, s_buf,
    qs, cs, qr, cr, co, vs, vr, vo, ls, lr, xs, xr,
    c_ss, c_rs, q_ss, q_rs, v_ss, v_rs, l_ss, l_rs, f_ss, f_rs, x_ss, x_rs, in_sem,
):
    me = lax.axis_index("dp")
    rep = lax.axis_index("rep")
    partner = (me, 1 - rep)
    rows, width = q_ref.shape
    slots = n * cap
    lanes = group * cap
    groups = n // group
    quarter = n // 4
    zone = me // quarter
    middle = (zone * (3 - zone)) // 2

    barrier = pltpu.get_barrier_semaphore()

    def greet(k, carry):
        pl.semaphore_signal(
            barrier, inc=1, device_id=(xor(me, k, n), rep), device_id_type=MESH
        )
        return carry

    lax.fori_loop(1, n, greet, 0)
    pl.semaphore_signal(barrier, inc=1, device_id=partner, device_id_type=MESH)

    b_in = pltpu.make_async_copy(b_hbm, b_ref, in_sem.at[0])
    c_in = pltpu.make_async_copy(c_hbm, c_ref, in_sem.at[1])
    q_in = pltpu.make_async_copy(q_hbm, q_ref, in_sem.at[2])
    b_in.start()
    c_in.start()
    q_in.start()
    b_in.wait()

    owner_col = lax.broadcasted_iota(jnp.int32, (n, rows), 0)
    chosen = owner_col == b_ref[...]
    hot = jnp.where(chosen, 1.0, 0.0)
    before = (
        lax.broadcasted_iota(jnp.int32, (rows, rows), 0)
        < lax.broadcasted_iota(jnp.int32, (rows, rows), 1)
    ).astype(jnp.bfloat16)
    dims = (((0,), (0,)), ((), ()))
    ahead = jnp.dot(hot.astype(jnp.bfloat16), before, preferred_element_type=jnp.float32)
    rank = jnp.sum(hot * ahead, axis=0, keepdims=True).astype(jnp.int32)
    hot_buf[...] = hot
    rank_buf[...] = rank
    slot_buf[...] = b_ref[...] * cap + rank
    vs[:, 0, :] = jnp.broadcast_to(jnp.sum(hot, axis=1, keepdims=True), (n, lanes))

    def remote(src, dst, ss, rs, device):
        return pltpu.make_async_remote_copy(
            src_ref=src, dst_ref=dst, send_sem=ss, recv_sem=rs,
            device_id=device, device_id_type=MESH,
        )

    def v_copy(o):
        return remote(vs.at[o], vr.at[me], v_ss.at[o], v_rs.at[me], (o, rep))

    def c_copy(o):
        return remote(cs.at[o], cr.at[me], c_ss.at[o], c_rs.at[me], (o, rep))

    def q_copy(o):
        return remote(qs.at[o], qr.at[me], q_ss.at[o], q_rs.at[me], (o, rep))

    def l_copy(o):
        return remote(ls.at[o // group], lr.at[me], l_ss.at[o], l_rs.at[me], (o, rep))

    def f_copy(o):
        return remote(cr.at[o], co.at[o], f_ss.at[o], f_rs.at[o], partner)

    def v_from(o):
        return remote(vs.at[me], vr.at[o], v_ss.at[o], v_rs.at[o], (o, rep))

    def c_from(o):
        return remote(cs.at[me], cr.at[o], c_ss.at[o], c_rs.at[o], (o, rep))

    def q_from(o):
        return remote(qs.at[me], qr.at[o], q_ss.at[o], q_rs.at[o], (o, rep))

    def l_from(o):
        return remote(ls.at[0], lr.at[o], l_ss.at[o], l_rs.at[o], (o, rep))

    within = lax.broadcasted_iota(jnp.int32, (cap, rows), 0)

    def pick(o, x_ref):
        taken = (slot_buf[...] == within + o * cap).astype(jnp.bfloat16)
        return jnp.dot(taken, x_ref[...], preferred_element_type=jnp.float32).astype(
            jnp.bfloat16
        )

    def peer(t):
        return xor(me, n - 1 - t, n)

    def arrival(u, size):
        return 4 * size - 1 - (u + (1 - middle) * 2 * size) % (3 * size)

    c_in.wait()
    cs[peer(0)] = pick(peer(0), c_ref)
    pl.semaphore_wait(barrier, n)

    def pack_c(t, carry):
        nxt = peer(t + 1)
        cs[nxt] = pick(nxt, c_ref)
        o = peer(t)
        c_copy(o).start()
        v_copy(o).start()
        return carry

    lax.fori_loop(0, n - 1, pack_c, 0)
    cr[me] = cs[me]
    vr[me] = vs[me]

    q_in.wait()
    qs[peer(0)] = pick(peer(0), q_ref)

    def pack_q(t, carry):
        nxt = peer(t + 1)
        qs[nxt] = pick(nxt, q_ref)
        q_copy(peer(t)).start()
        return carry

    lax.fori_loop(0, n - 1, pack_q, 0)
    qr[me] = qs[me]
    f_copy(me).start()

    row_at = lax.broadcasted_iota(jnp.int32, (cap, lanes), 0)
    lane_at = lax.broadcasted_iota(jnp.int32, (cap, lanes), 1)
    row_number = row_at.astype(jnp.float32)

    def fill_bias(number, at):
        bias_buf[pl.ds(pl.multiple_of(at, cap), cap), :] = jnp.where(
            row_number < number, 0.0, neg_large
        )

    def forward(o):
        c_from(o).wait_recv()
        f_copy(o).start()
        v_from(o).wait_recv()

    lax.fori_loop(1, quarter, lambda k, c: (forward(xor(me, k, n)), c)[1], 0)
    lax.fori_loop(
        0, 3 * quarter, lambda u, c: (forward(xor(me, arrival(u, quarter), n)), c)[1], 0
    )
    v_forward = remote(vr, vo, x_ss.at[0], x_rs.at[0], partner)
    v_forward.start()
    lax.fori_loop(0, n, lambda j, c: (fill_bias(vr[j], j * cap), c)[1], 0)
    v_forward.wait_recv()
    lax.fori_loop(0, n, lambda j, c: (fill_bias(vo[j], (n + j) * cap), c)[1], 0)
    count = jnp.sum(vr[:, 0, :], axis=0, keepdims=True) + jnp.sum(
        vo[:, 0, :], axis=0, keepdims=True
    )
    count_safe = jnp.maximum(count, 1.0)
    log_count = jnp.log(count_safe)
    lax.fori_loop(0, n, lambda j, c: (f_copy(j).wait_recv(), c)[1], 0)

    chunk = math.gcd(slots, 256)
    one_row = lax.broadcasted_iota(jnp.int32, (1, lanes), 1)

    def group_loss(p):
        block = qr[pl.ds(p * group, group)].reshape(lanes, width)
        top = jnp.full((8, lanes), neg_large, jnp.float32)
        for half, held in enumerate((cr, co)):
            flat = held.reshape(slots, width)
            for start in range(0, slots, chunk):
                at = half * slots + start
                scores = lax.dot_general(
                    flat[start : start + chunk, :], block,
                    (((1,), (1,)), ((), ())), preferred_element_type=jnp.float32,
                ) + bias_buf[at : at + chunk, :]
                s_buf[at : at + chunk, :] = scores
                top = jnp.maximum(top, jnp.max(scores.reshape(chunk // 8, 8, lanes), axis=0))
        peak = jnp.max(top, axis=0, keepdims=True)
        total = jnp.zeros((8, lanes), jnp.float32)
        for at in range(0, 2 * slots, chunk):
            powers = jnp.exp2((s_buf[at : at + chunk, :] - peak) * (score_scale * log2e))
            total = total + jnp.sum(powers.reshape(chunk // 8, 8, lanes), axis=0)
        lse = peak * score_scale + jnp.log(jnp.sum(total, axis=0, keepdims=True))
        positive = jnp.zeros((1, lanes), jnp.float32)
        keep = jnp.zeros((1, lanes), jnp.float32)
        for g in range(group):
            j = p * group + g
            own = s_buf[pl.ds(pl.multiple_of(j * cap, cap), cap), :]
            positive = positive + jnp.sum(
                jnp.where(row_at == lane_at - g * cap, own, 0.0), axis=0, keepdims=True
            )
            place = one_row - g * cap
            here = jnp.logical_and(place >= 0, place.astype(jnp.float32) < vr[j])
            here = jnp.logical_and(here, place < cap)
            keep = jnp.where(here, 1.0, keep)
        loss = (lse - positive * score_scale) - log_count
        return jnp.where(keep > 0.0, loss, 0.0)

    def step(m, total):
        p = xor(me // group, m, groups)
        for g in range(group):
            j = p * group + g

            @pl.when(j != me)
            def _():
                q_from(j).wait_recv()

        row = group_loss(p)
        ls[p] = row
        total = total + row
        xs[...] = total
        for g in range(group):
            j = p * group + g

            @pl.when(j != me)
            def _():
                l_copy(j).start()

        return total

    part = groups // 4
    total = lax.fori_loop(0, part, step, jnp.zeros((1, lanes), jnp.float32))
    total = lax.fori_loop(0, 3 * part, lambda u, c: step(arrival(u, part), c), total)
    lr[me] = ls[me // group]
    x_copy = remote(xs, xr, x_ss.at[1], x_rs.at[1], partner)
    x_copy.start()

    def close(t, carry):
        o = xor(me, n - 1 - t, n)
        c_copy(o).wait_send()
        q_copy(o).wait_send()
        v_copy(o).wait_send()
        l_copy(o).wait_send()
        f_copy(o).wait_send()
        l_from(o).wait_recv()
        return carry

    lax.fori_loop(0, n - 1, close, 0)
    f_copy(me).wait_send()
    v_forward.wait_send()

    spread_loss = lax.dot_general(
        lr[:, 0, :], hot_buf[...], dims,
        precision=lax.Precision.HIGHEST, preferred_element_type=jnp.float32,
    )
    mine = lax.broadcasted_iota(jnp.int32, (lanes, rows), 0) == rank_buf[...] + (me % group) * cap
    ql_ref[...] = jnp.sum(jnp.where(mine, spread_loss, 0.0), axis=0)
    x_copy.wait()
    summed = jnp.sum(total + xr[...], axis=1, keepdims=True)
    bl_ref[...] = (summed / count_safe)[:, :128]


def shards(queries, candidates, bucket):
    n = lax.axis_size("dp")
    rows, width = queries.shape
    cap = max(2, 2 * rows // n)
    cap = (cap + 15) // 16 * 16
    group = 1
    while 2 * group * cap <= 256 and n % (8 * group) == 0:
        group *= 2
    slots, lanes = n * cap, group * cap
    bf16, f32 = jnp.bfloat16, jnp.float32
    vmem = pl.BlockSpec(memory_space=pltpu.VMEM)
    dma = pltpu.SemaphoreType.DMA
    query_loss, bucket_loss = pl.pallas_call(
        functools.partial(kernel, n, cap, group),
        out_shape=(
            pltpu.VMEM((rows,), f32),
            pltpu.VMEM((1, 128), f32),
        ),
        in_specs=[pl.BlockSpec(memory_space=pl.ANY)] * 3,
        out_specs=(vmem, vmem),
        scratch_shapes=[
            pltpu.VMEM((1, rows), jnp.int32),
            pltpu.VMEM((rows, width), bf16),
            pltpu.VMEM((rows, width), bf16),
            pltpu.VMEM((1, rows), jnp.int32),
            pltpu.VMEM((n, rows), f32),
            pltpu.VMEM((1, rows), jnp.int32),
            pltpu.VMEM((2 * slots, lanes), f32),
            pltpu.VMEM((2 * slots, lanes), f32),
        ]
        + [pltpu.VMEM((n, cap, width), bf16)] * 5
        + [pltpu.VMEM((n, 1, lanes), f32)] * 3
        + [pltpu.VMEM((n // group, 1, lanes), f32), pltpu.VMEM((n, 1, lanes), f32)]
        + [pltpu.VMEM((1, lanes), f32)] * 2
        + [dma((n,))] * 10
        + [dma((2,))] * 2
        + [dma((3,))],
        compiler_params=pltpu.CompilerParams(collective_id=0, has_side_effects=True),
        name="bucket_loss",
    )(bucket.reshape(1, rows), queries, candidates)
    return query_loss, bucket_loss[0, :1]


def solution(mesh):
    in_specs = (P(("dp", "rep"), None), P(("dp", "rep"), None), P(("dp", "rep"), None))
    out_specs = (P(("dp", "rep")), P("dp"))
    return jax.shard_map(shards, mesh=mesh, in_specs=in_specs, out_specs=out_specs, check_vma=False)
```

```python
import functools
import math

import jax
import jax.numpy as jnp
from jax import lax
from jax.experimental import pallas as pl
from jax.experimental.pallas import tpu as pltpu
from jax.sharding import PartitionSpec as P

MESH = pl.DeviceIdType.MESH
score_scale = 0.0625
neg_large = -1e30
log2e = math.log2(math.e)


def xor(a, b, n):
    out, bit = 0, 1
    while bit < n:
        out = out + bit * ((a // bit + b // bit) % 2)
        bit *= 2
    return out


def kernel(
    n, cap, group, b_hbm, q_hbm, c_hbm, ql_ref, bl_ref, b_ref, q_ref, c_ref,
    slot_buf, hot_buf, rank_buf, bias_buf, s_buf,
    qs, cs, qr, cr, co, vs, vr, vo, ls, lr, xs, xr,
    c_ss, c_rs, q_ss, q_rs, v_ss, v_rs, l_ss, l_rs, f_ss, f_rs, x_ss, x_rs, in_sem,
):
    me = lax.axis_index("dp")
    rep = lax.axis_index("rep")
    partner = (me, 1 - rep)
    rows, width = q_ref.shape
    slots = n * cap
    lanes = group * cap
    groups = n // group
    quarter = n // 4
    zone = me // quarter
    middle = (zone * (3 - zone)) // 2

    barrier = pltpu.get_barrier_semaphore()

    def greet(k, carry):
        pl.semaphore_signal(
            barrier, inc=1, device_id=((me + k) % n, rep), device_id_type=MESH
        )
        return carry

    lax.fori_loop(1, n, greet, 0)
    pl.semaphore_signal(barrier, inc=1, device_id=partner, device_id_type=MESH)

    b_in = pltpu.make_async_copy(b_hbm, b_ref, in_sem.at[0])
    c_in = pltpu.make_async_copy(c_hbm, c_ref, in_sem.at[1])
    q_in = pltpu.make_async_copy(q_hbm, q_ref, in_sem.at[2])
    b_in.start()
    c_in.start()
    q_in.start()
    b_in.wait()

    owner_col = lax.broadcasted_iota(jnp.int32, (n, rows), 0)
    chosen = owner_col == b_ref[...]
    hot = jnp.where(chosen, 1.0, 0.0)
    before = (
        lax.broadcasted_iota(jnp.int32, (rows, rows), 0)
        < lax.broadcasted_iota(jnp.int32, (rows, rows), 1)
    ).astype(jnp.bfloat16)
    dims = (((0,), (0,)), ((), ()))
    ahead = jnp.dot(hot.astype(jnp.bfloat16), before, preferred_element_type=jnp.float32)
    rank = jnp.sum(hot * ahead, axis=0, keepdims=True).astype(jnp.int32)
    hot_buf[...] = hot
    rank_buf[...] = rank
    slot_buf[...] = b_ref[...] * cap + rank
    vs[:, 0, :] = jnp.broadcast_to(jnp.sum(hot, axis=1, keepdims=True), (n, lanes))

    def remote(src, dst, ss, rs, device):
        return pltpu.make_async_remote_copy(
            src_ref=src, dst_ref=dst, send_sem=ss, recv_sem=rs,
            device_id=device, device_id_type=MESH,
        )

    def v_copy(o):
        return remote(vs.at[o], vr.at[me], v_ss.at[o], v_rs.at[me], (o, rep))

    def c_copy(o):
        return remote(cs.at[o], cr.at[me], c_ss.at[o], c_rs.at[me], (o, rep))

    def q_copy(o):
        return remote(qs.at[o], qr.at[me], q_ss.at[o], q_rs.at[me], (o, rep))

    def l_copy(o):
        return remote(ls.at[o // group], lr.at[me], l_ss.at[o], l_rs.at[me], (o, rep))

    def f_copy(o):
        return remote(cr.at[o], co.at[o], f_ss.at[o], f_rs.at[o], partner)

    def v_from(o):
        return remote(vs.at[me], vr.at[o], v_ss.at[o], v_rs.at[o], (o, rep))

    def c_from(o):
        return remote(cs.at[me], cr.at[o], c_ss.at[o], c_rs.at[o], (o, rep))

    def q_from(o):
        return remote(qs.at[me], qr.at[o], q_ss.at[o], q_rs.at[o], (o, rep))

    def l_from(o):
        return remote(ls.at[0], lr.at[o], l_ss.at[o], l_rs.at[o], (o, rep))

    within = lax.broadcasted_iota(jnp.int32, (cap, rows), 0)

    def pick(o, x_ref):
        taken = (slot_buf[...] == within + o * cap).astype(jnp.bfloat16)
        return jnp.dot(taken, x_ref[...], preferred_element_type=jnp.float32).astype(
            jnp.bfloat16
        )

    def peer(t):
        return xor(me, n - 1 - t, n)

    def arrival(u, size):
        return 4 * size - 1 - (u + (1 - middle) * 2 * size) % (3 * size)

    c_in.wait()
    cs[peer(0)] = pick(peer(0), c_ref)
    pl.semaphore_wait(barrier, n)

    def pack_c(t, carry):
        nxt = peer(t + 1)
        cs[nxt] = pick(nxt, c_ref)
        o = peer(t)
        c_copy(o).start()
        v_copy(o).start()
        return carry

    lax.fori_loop(0, n - 1, pack_c, 0)
    cr[me] = cs[me]
    vr[me] = vs[me]

    q_in.wait()
    qs[peer(0)] = pick(peer(0), q_ref)

    def pack_q(t, carry):
        nxt = peer(t + 1)
        qs[nxt] = pick(nxt, q_ref)
        q_copy(peer(t)).start()
        return carry

    lax.fori_loop(0, n - 1, pack_q, 0)
    qr[me] = qs[me]
    f_copy(me).start()

    row_at = lax.broadcasted_iota(jnp.int32, (cap, lanes), 0)
    lane_at = lax.broadcasted_iota(jnp.int32, (cap, lanes), 1)
    row_number = row_at.astype(jnp.float32)

    def fill_bias(number, at):
        bias_buf[pl.ds(pl.multiple_of(at, cap), cap), :] = jnp.where(
            row_number < number, 0.0, neg_large
        )

    def forward(o):
        c_from(o).wait_recv()
        f_copy(o).start()
        v_from(o).wait_recv()

    lax.fori_loop(1, quarter, lambda k, c: (forward(xor(me, k, n)), c)[1], 0)
    lax.fori_loop(
        0, 3 * quarter, lambda u, c: (forward(xor(me, arrival(u, quarter), n)), c)[1], 0
    )
    v_forward = remote(vr, vo, x_ss.at[0], x_rs.at[0], partner)
    v_forward.start()
    lax.fori_loop(0, n, lambda j, c: (fill_bias(vr[j], j * cap), c)[1], 0)
    v_forward.wait_recv()
    lax.fori_loop(0, n, lambda j, c: (fill_bias(vo[j], (n + j) * cap), c)[1], 0)
    count = jnp.sum(vr[:, 0, :], axis=0, keepdims=True) + jnp.sum(
        vo[:, 0, :], axis=0, keepdims=True
    )
    count_safe = jnp.maximum(count, 1.0)
    log_count = jnp.log(count_safe)
    lax.fori_loop(0, n, lambda j, c: (f_copy(j).wait_recv(), c)[1], 0)

    def sent(t, carry):
        o = (me + 1 + t) % n
        c_copy(o).wait_send()
        v_copy(o).wait_send()
        f_copy(o).wait_send()
        return carry

    lax.fori_loop(0, n - 1, sent, 0)
    f_copy(me).wait_send()
    v_forward.wait_send()

    chunk = math.gcd(slots, 256)
    one_row = lax.broadcasted_iota(jnp.int32, (1, lanes), 1)

    def group_loss(p):
        block = qr[pl.ds(p * group, group)].reshape(lanes, width)
        top = jnp.full((8, lanes), neg_large, jnp.float32)
        for half, held in enumerate((cr, co)):
            flat = held.reshape(slots, width)
            for start in range(0, slots, chunk):
                at = half * slots + start
                scores = lax.dot_general(
                    flat[start : start + chunk, :], block,
                    (((1,), (1,)), ((), ())), preferred_element_type=jnp.float32,
                ) + bias_buf[at : at + chunk, :]
                s_buf[at : at + chunk, :] = scores
                top = jnp.maximum(top, jnp.max(scores.reshape(chunk // 8, 8, lanes), axis=0))
        peak = jnp.max(top, axis=0, keepdims=True)
        total = jnp.zeros((8, lanes), jnp.float32)
        for at in range(0, 2 * slots, chunk):
            powers = jnp.exp2((s_buf[at : at + chunk, :] - peak) * (score_scale * log2e))
            total = total + jnp.sum(powers.reshape(chunk // 8, 8, lanes), axis=0)
        lse = peak * score_scale + jnp.log(jnp.sum(total, axis=0, keepdims=True))
        positive = jnp.zeros((1, lanes), jnp.float32)
        keep = jnp.zeros((1, lanes), jnp.float32)
        for g in range(group):
            j = p * group + g
            own = s_buf[pl.ds(pl.multiple_of(j * cap, cap), cap), :]
            positive = positive + jnp.sum(
                jnp.where(row_at == lane_at - g * cap, own, 0.0), axis=0, keepdims=True
            )
            place = one_row - g * cap
            here = jnp.logical_and(place >= 0, place.astype(jnp.float32) < vr[j])
            here = jnp.logical_and(here, place < cap)
            keep = jnp.where(here, 1.0, keep)
        loss = (lse - positive * score_scale) - log_count
        return jnp.where(keep > 0.0, loss, 0.0)

    def step(m, total):
        p = xor(me // group, m, groups)
        for g in range(group):
            j = p * group + g

            @pl.when(j != me)
            def _():
                q_from(j).wait_recv()

        row = group_loss(p)
        ls[p] = row
        total = total + row
        xs[...] = total
        for g in range(group):
            j = p * group + g

            @pl.when(j != me)
            def _():
                l_copy(j).start()

        return total

    part = groups // 4
    total = lax.fori_loop(0, part, step, jnp.zeros((1, lanes), jnp.float32))
    total = lax.fori_loop(0, 3 * part, lambda u, c: step(arrival(u, part), c), total)
    lr[me] = ls[me // group]
    x_copy = remote(xs, xr, x_ss.at[1], x_rs.at[1], partner)
    x_copy.start()

    def close(t, carry):
        o = (me + 1 + t) % n
        q_copy(o).wait_send()
        l_copy(o).wait_send()
        l_from(o).wait_recv()
        return carry

    lax.fori_loop(0, n - 1, close, 0)

    spread_loss = lax.dot_general(
        lr[:, 0, :], hot_buf[...], dims,
        precision=lax.Precision.HIGHEST, preferred_element_type=jnp.float32,
    )
    mine = lax.broadcasted_iota(jnp.int32, (lanes, rows), 0) == rank_buf[...] + (me % group) * cap
    ql_ref[...] = jnp.sum(jnp.where(mine, spread_loss, 0.0), axis=0)
    x_copy.wait()
    summed = jnp.sum(total + xr[...], axis=1, keepdims=True)
    bl_ref[...] = (summed / count_safe)[:, :128]


def shards(queries, candidates, bucket):
    n = lax.axis_size("dp")
    rows, width = queries.shape
    cap = max(2, 2 * rows // n)
    cap = (cap + 15) // 16 * 16
    group = 1
    while 2 * group * cap <= 256 and n % (8 * group) == 0:
        group *= 2
    slots, lanes = n * cap, group * cap
    bf16, f32 = jnp.bfloat16, jnp.float32
    vmem = pl.BlockSpec(memory_space=pltpu.VMEM)
    dma = pltpu.SemaphoreType.DMA
    query_loss, bucket_loss = pl.pallas_call(
        functools.partial(kernel, n, cap, group),
        out_shape=(
            pltpu.VMEM((rows,), f32),
            pltpu.VMEM((1, 128), f32),
        ),
        in_specs=[pl.BlockSpec(memory_space=pl.ANY)] * 3,
        out_specs=(vmem, vmem),
        scratch_shapes=[
            pltpu.VMEM((1, rows), jnp.int32),
            pltpu.VMEM((rows, width), bf16),
            pltpu.VMEM((rows, width), bf16),
            pltpu.VMEM((1, rows), jnp.int32),
            pltpu.VMEM((n, rows), f32),
            pltpu.VMEM((1, rows), jnp.int32),
            pltpu.VMEM((2 * slots, lanes), f32),
            pltpu.VMEM((2 * slots, lanes), f32),
        ]
        + [pltpu.VMEM((n, cap, width), bf16)] * 5
        + [pltpu.VMEM((n, 1, lanes), f32)] * 3
        + [pltpu.VMEM((n // group, 1, lanes), f32), pltpu.VMEM((n, 1, lanes), f32)]
        + [pltpu.VMEM((1, lanes), f32)] * 2
        + [dma((n,))] * 10
        + [dma((2,))] * 2
        + [dma((3,))],
        compiler_params=pltpu.CompilerParams(collective_id=0, has_side_effects=True),
        name="bucket_loss",
    )(bucket.reshape(1, rows), queries, candidates)
    return query_loss, bucket_loss[0, :1]


def solution(mesh):
    in_specs = (P(("dp", "rep"), None), P(("dp", "rep"), None), P(("dp", "rep"), None))
    out_specs = (P(("dp", "rep")), P("dp"))
    return jax.shard_map(shards, mesh=mesh, in_specs=in_specs, out_specs=out_specs, check_vma=False)
```
